128 devices in a mesh: tok: 8 (over x, core), voc: 16 (over z, y).
Axes of the slice: x: 4, y: 4, z: 4, core: 2. Of those that a mesh axis runs over, the one named last changes fastest.
Arguments:
- hidden: bfloat16 [256, 32, 2048], P(('tok', 'voc')), may hold values from -40 to 40
- norm_gain: float32 [2048], replicated, may hold values from 0.5 to 1.5
- head_weight: bfloat16 [2048, 102400], P(None, 'voc'), may hold values from -2 to 2
- lengths: int32 [256], P(('tok', 'voc')), may hold values from 12 to 24, as said below
- offsets: int32 [256], P(('tok', 'voc')), may hold values from 0 to 8
- slot_request: int32 [256], replicated, may hold values from 0 to 255, each once
- targets: int32 [256, 32], P(('tok', 'voc')), may hold values from 0 to 102399
Outputs:
- token_logprob: float32 [256, 32], P(('tok', 'voc'))
- token_entropy: float32 [256, 32], P(('tok', 'voc'))
The draws below stay inside these ranges and needn't reach their ends.
Inputs may be any that keep to these rules, and one draw needn't show every extreme that they name: `lengths`: each request has 12 to 24 response rows; all 2 requests of some one scoring device have exactly 24. Response rows end within the window: offsets + lengths <= 32. `slot_request`: every request appears in exactly one slot.
All inputs are finite; a program needn't handle non-finite values.
Results may differ from the reference program's by a relative error of at most 0.00145.
Values may be sent and summed in bfloat16 or wider, within the bound.
A program may use at most 128 MiB of HBM per device.

```python
import jax
import jax.numpy as jnp
from jax import lax

D = 2048
SPAN = 32
LIVE = 24
REQ_DEV = 2
VOCAB = 102400
REQS = 256
N_VOC = 16


def special_columns(key):
    columns = jax.random.permutation(jax.random.fold_in(key, 31), VOCAB)[:6]
    vectors = jnp.clip(jax.random.normal(jax.random.fold_in(key, 32), (D, 3), jnp.float32), -3.0, 3.0)
    return (columns, vectors)


def draw_head_weight(key, part):
    weight = jnp.clip(jax.random.normal(jax.random.fold_in(key, 33), (D, VOCAB), jnp.float32), -5.0, 5.0) * (3.2 * D ** (-0.5))
    columns, vectors = special_columns(key)
    strength = jnp.array([2.5, 5.0, 7.5], jnp.float32)
    factor = 40.0 / D
    weight = weight.at[:, columns[:3]].set(vectors * strength[None, :] * factor)
    weight = weight.at[:, columns[3:]].set(vectors * (strength[None, :] - 0.05) * factor)
    return weight.astype(jnp.bfloat16)


def draw_hidden(key, part):
    values = jnp.clip(jax.random.normal(jax.random.fold_in(key, 21), (REQS, SPAN, D), jnp.float32), -6.0, 6.0)
    columns, vectors = special_columns(key)
    count = min(48, REQS * SPAN)
    planted_at = jax.random.permutation(jax.random.fold_in(key, 25), REQS * SPAN)[:count]
    which = jnp.arange(count) % 3
    noise = jax.random.normal(jax.random.fold_in(key, 26), (count, D), jnp.float32) * 0.01
    planted = vectors.T[which] + noise
    values = values.reshape(REQS * SPAN, D).at[planted_at].set(planted).reshape(REQS, SPAN, D)
    return values.astype(jnp.bfloat16)


def draw_lengths(key, part):
    drawn = jax.random.randint(jax.random.fold_in(key, 41), (REQS,), LIVE // 2, LIVE + 1)
    chosen = jax.random.randint(jax.random.fold_in(key, 42), (), 0, REQS // REQ_DEV)
    owners = jnp.arange(REQS, dtype=jnp.int32) // REQ_DEV
    return jnp.where(owners == chosen, LIVE, drawn).astype(jnp.int32)


def with_ends(entries, key, smallest, largest):
    place = [jax.random.randint(jax.random.fold_in(key, axis), (), 0, length) for axis, length in enumerate(entries.shape)]
    main_axis = entries.shape.index(max(entries.shape))
    beside = place[:main_axis] + [(place[main_axis] + 1) % entries.shape[main_axis]] + place[main_axis + 1:]
    return entries.at[tuple(place)].set(smallest).at[tuple(beside)].set(largest)


def setup_inputs(seed: int = 0) -> dict:
    keys = jax.random.split(jax.random.key(seed), 8)
    return {
        "hidden": draw_hidden(jax.random.fold_in(keys[7], 71), 0),
        "norm_gain": jnp.clip(1.0 + 0.1 * jax.random.normal(keys[1], (D,), jnp.float32), 0.5, 1.5),
        "head_weight": draw_head_weight(jax.random.fold_in(keys[7], 71), 0),
        "lengths": draw_lengths(jax.random.fold_in(keys[7], 71), 0),
        "offsets": with_ends(jax.random.randint(keys[4], (REQS,), 0, SPAN - LIVE + 1), jax.random.fold_in(keys[4], 1), 0, SPAN - LIVE).astype(jnp.int32),
        "slot_request": jax.random.permutation(keys[5], REQS).astype(jnp.int32),
        "targets": with_ends(jax.random.randint(keys[6], (REQS, SPAN), 0, VOCAB), jax.random.fold_in(keys[6], 1), 0, VOCAB - 1).astype(jnp.int32),
    }


EPS = 1e-06

def normalize(hidden, norm_gain):
    values = hidden.astype(jnp.float32)
    square = lax.optimization_barrier(jnp.mean(values * values, axis=-1, keepdims=True))
    return (values * lax.rsqrt(square + EPS) * norm_gain.astype(jnp.float32)).astype(jnp.bfloat16)

def reference(hidden, norm_gain, head_weight, lengths, offsets, slot_request, targets):
    normed = normalize(hidden, norm_gain)
    block = N_VOC * REQ_DEV * SPAN
    block_rows = normed.reshape(-1, block, D)
    block_goals = targets.reshape(-1, block)

    def one_block(item):
        rows_here, goals_here = item
        logits = jnp.dot(rows_here, head_weight, preferred_element_type=jnp.float32)
        row_peak = lax.optimization_barrier(jnp.max(logits, axis=1))
        scaled = jnp.exp(logits - row_peak[:, None])
        exp_sum = lax.optimization_barrier(jnp.sum(scaled, axis=1))
        exp_dot = lax.optimization_barrier(jnp.sum(scaled * logits, axis=1))
        picked = jnp.take_along_axis(logits, goals_here[:, None].astype(jnp.int32), axis=1)[:, 0]
        return (row_peak, exp_sum, exp_dot, picked)
    row_peak, exp_sum, exp_dot, picked = lax.map(one_block, (block_rows, block_goals))
    row_peak = row_peak.reshape(REQS, SPAN)
    exp_sum = exp_sum.reshape(REQS, SPAN)
    exp_dot = exp_dot.reshape(REQS, SPAN)
    picked = picked.reshape(REQS, SPAN)
    position = jnp.arange(SPAN, dtype=jnp.int32)[None, :]
    in_span = (position >= offsets[:, None]) & (position < offsets[:, None] + lengths[:, None])
    log_total = jnp.log(exp_sum)
    scored_logprob = jnp.where(in_span, picked - row_peak - log_total, 0.0)
    scored_entropy = jnp.where(in_span, row_peak + log_total - exp_dot / exp_sum, 0.0)
    token_logprob = jnp.zeros_like(scored_logprob).at[slot_request].set(scored_logprob)
    token_entropy = jnp.zeros_like(scored_entropy).at[slot_request].set(scored_entropy)
    return (token_logprob, token_entropy)
```

```python
import functools

import jax
import jax.numpy as jnp
from jax import lax
from jax.experimental import pallas as pl
from jax.experimental.pallas import tpu as pltpu
from jax.sharding import PartitionSpec as P

EPS = 1e-06
LIVE = 24
SIDE = 4
LOW = -1e30
MESH = pl.DeviceIdType.MESH


def kernel(
    n_tok, columns,
    hidden_ref, gain_ref, targets_ref, lengths_ref, offsets_ref, request_ref, weight_hbm,
    logprob_ref, entropy_ref,
    normed_ref, rows_ref, meta_ref, weight_ref, even_ref, odd_ref,
    peak_ref, sum_ref, dot_ref, pick_ref, goal_ref,
    stat_ref, every_ref, code_ref, final_ref, owner_ref,
    weight_sem, row_send, row_recv, meta_send, meta_recv,
    stat_send, stat_recv, owner_send, owner_recv, final_send, final_recv,
):
    req_dev, span, width = hidden_ref.shape
    vocab_dev = weight_hbm.shape[1]
    chunks = vocab_dev // columns
    shard_rows = req_dev * LIVE
    tok, voc = lax.axis_index("tok"), lax.axis_index("voc")
    core = lax.rem(tok, 2)
    high, low = voc // SIDE, lax.rem(voc, SIDE)
    a = low + core * (high - low)
    b = high + core * (low - high)

    def shard_of(b_at, a_at):
        high_at = b_at + core * (a_at - b_at)
        low_at = a_at + core * (b_at - a_at)
        return high_at * SIDE + low_at

    def ring(place, step):
        return lax.rem(place + step + SIDE, SIDE)

    a_next, a_prev, a_far = ring(a, 1), ring(a, -1), ring(a, 2)
    b_next, b_prev, b_far = ring(b, 1), ring(b, -1), ring(b, 2)
    mine = b * SIDE + a

    weight_copies = [
        pltpu.make_async_copy(weight_hbm.at[:, pl.ds(c * columns, columns)], weight_ref.at[c], weight_sem.at[c])
        for c in range(chunks)
    ]
    for copy in weight_copies:
        copy.start()

    barrier = pltpu.get_barrier_semaphore()
    to_a_next, to_a_prev = (tok, shard_of(b, a_next)), (tok, shard_of(b, a_prev))
    to_b_next, to_b_prev = (tok, shard_of(b_next, a)), (tok, shard_of(b_prev, a))
    for peer in (to_a_next, to_a_prev, to_b_next, to_b_prev):
        pl.semaphore_signal(barrier, inc=1, device_id=peer, device_id_type=MESH)
    for step in range(1, n_tok):
        pl.semaphore_signal(barrier, inc=1, device_id=(lax.rem(tok + step, n_tok), voc), device_id_type=MESH)

    lane = lax.broadcasted_iota(jnp.int32, (1, 128), 1)
    which = lax.rem(lane // span, req_dev)
    own_half = lane // (req_dev * span) == lax.rem(a, 2)
    offset = jnp.where(which == 0, offsets_ref[0], offsets_ref[1])
    length = jnp.where(which == 0, lengths_ref[0], lengths_ref[1])
    relative = lax.rem(lane, span) - offset
    alive = own_half & (relative >= 0) & (relative < length)
    code = jnp.where(alive, (lane // span) * span + relative + 1, 0)
    first_slot = (tok * SIDE * SIDE + voc) * req_dev
    request = jnp.where(own_half, jnp.where(which == 0, request_ref[first_slot], request_ref[first_slot + 1]), 0)
    goals = targets_ref[...]
    goals = jnp.concatenate([goals[0:1], goals[1:2], goals[0:1], goals[1:2]], axis=1)
    goals = jnp.where(own_half, goals, 0)
    meta_ref[b, a] = jnp.concatenate(
        [goals.astype(jnp.float32), code.astype(jnp.float32), request.astype(jnp.float32), jnp.zeros((5, 128), jnp.float32)], axis=0
    )

    for j in range(req_dev):
        values = hidden_ref[j].astype(jnp.float32)
        square = jnp.mean(values * values, axis=-1, keepdims=True)
        normed_ref[pl.ds(j * span, span), :] = (values * lax.rsqrt(square + EPS) * gain_ref[...]).astype(jnp.bfloat16)
    row = lax.broadcasted_iota(jnp.int32, (shard_rows, req_dev * span), 0)
    column = lax.broadcasted_iota(jnp.int32, (shard_rows, req_dev * span), 1)
    source = jnp.where(row < LIVE, row + offsets_ref[0], row - LIVE + span + offsets_ref[1])
    chosen = jnp.where(source == column, 1.0, 0.0).astype(jnp.bfloat16)
    own_rows = pl.ds(pl.multiple_of(a * shard_rows, shard_rows), shard_rows)
    rows_ref[b, own_rows, :] = jnp.dot(chosen, normed_ref[...], preferred_element_type=jnp.float32).astype(jnp.bfloat16)

    pl.semaphore_wait(barrier, 4 + n_tok - 1)

    def send(ref, index, sems, place, peer):
        copy = pltpu.make_async_remote_copy(
            src_ref=ref.at[index], dst_ref=ref.at[index], send_sem=sems[0].at[place], recv_sem=sems[1].at[place],
            device_id=peer, device_id_type=MESH,
        )
        copy.start()
        return copy

    row_sems, meta_sems = (row_send, row_recv), (meta_send, meta_recv)
    whole, left, right = pl.ds(0, width), pl.ds(0, width // 2), pl.ds(width // 2, width // 2)

    def rows_at(b_at, a_at, part):
        return (b_at, pl.ds(pl.multiple_of(a_at * shard_rows, shard_rows), shard_rows), part)

    def landed(ref, index, sems, place):
        pltpu.make_async_copy(ref.at[index], ref.at[index], sems[1].at[place]).wait()

    sends = []
    sends.append(send(rows_ref, rows_at(b, a, whole), row_sems, 0, to_a_next))
    sends.append(send(rows_ref, rows_at(b, a, whole), row_sems, 1, to_a_prev))
    sends.append(send(meta_ref, (b, a), meta_sems, 0, to_a_next))
    sends.append(send(meta_ref, (b, a), meta_sems, 1, to_a_prev))
    landed(rows_ref, rows_at(b, a_prev, whole), row_sems, 0)
    sends.append(send(rows_ref, rows_at(b, a_prev, left), row_sems, 2, to_a_next))
    landed(meta_ref, (b, a_prev), meta_sems, 0)
    sends.append(send(meta_ref, (b, a_prev), meta_sems, 2, to_a_next))
    landed(rows_ref, rows_at(b, a_next, whole), row_sems, 1)
    sends.append(send(rows_ref, rows_at(b, a_next, right), row_sems, 3, to_a_prev))
    landed(meta_ref, (b, a_next), meta_sems, 1)
    for k, a_at in enumerate((a, a_prev, a_next)):
        sends.append(send(rows_ref, rows_at(b, a_at, whole), row_sems, 4 + 2 * k, to_b_next))
        sends.append(send(rows_ref, rows_at(b, a_at, whole), row_sems, 5 + 2 * k, to_b_prev))
    landed(rows_ref, rows_at(b, a_far, left), row_sems, 2)
    landed(rows_ref, rows_at(b, a_far, right), row_sems, 3)
    landed(meta_ref, (b, a_far), meta_sems, 2)
    sends.append(send(rows_ref, rows_at(b, a_far, whole), row_sems, 10, to_b_next))
    sends.append(send(rows_ref, rows_at(b, a_far, whole), row_sems, 11, to_b_prev))
    sends.append(send(meta_ref, (b,), meta_sems, 3, to_b_next))
    sends.append(send(meta_ref, (b,), meta_sems, 4, to_b_prev))

    lines = (b, b_next, b_prev, b_far)
    buffers = (even_ref, odd_ref)
    sub_row = lax.broadcasted_iota(jnp.int32, (128, 128), 0).astype(jnp.float32) + 1.0
    sub_lane = lax.broadcasted_iota(jnp.int32, (128, 128), 1)

    def begin(line):
        peak_ref[...] = jnp.full_like(peak_ref, LOW)
        sum_ref[...] = jnp.zeros_like(sum_ref)
        dot_ref[...] = jnp.zeros_like(dot_ref)
        pick_ref[...] = jnp.zeros_like(pick_ref)
        for half in range(2):
            both = meta_ref[line, 2 * half] + meta_ref[line, 2 * half + 1]
            goal = jnp.sum(jnp.where(both[1:2] == sub_row, both[0:1], 0.0), axis=1, keepdims=True)
            goal_ref[pl.ds(half * 128, 128), :] = goal.astype(jnp.int32) - voc * vocab_dev - sub_lane

    def multiply(line, chunk, buffer):
        buffer[...] = jnp.dot(rows_ref[line], weight_ref[chunk], preferred_element_type=jnp.float32)

    def collect(chunk, buffer):
        for group in range(SIDE * shard_rows // 8):
            request_at, part = group // 3, group % 3
            at = pl.ds(request_at * span + part * 8, 8)
            logits = [buffer[pl.ds(group * 8, 8), pl.ds(c * 128, 128)] for c in range(columns // 128)]
            peak = peak_ref[at]
            top = functools.reduce(jnp.maximum, logits, peak)
            rescale = jnp.exp(peak - top)
            exp_sum, exp_dot = sum_ref[at] * rescale, dot_ref[at] * rescale
            picked, goal = pick_ref[at], goal_ref[at]
            for c, logit in enumerate(logits):
                scaled = jnp.exp(logit - top)
                exp_sum = exp_sum + scaled
                exp_dot = exp_dot + scaled * logit
                picked = jnp.where(goal == chunk * columns + c * 128, logit, picked)
            peak_ref[at], sum_ref[at], dot_ref[at], pick_ref[at] = top, exp_sum, exp_dot, picked

    def finish(line):
        for half in range(2):
            at = pl.ds(half * 128, 128)
            peak = peak_ref[at].T
            top = jnp.max(peak, axis=0, keepdims=True)
            rescale = jnp.exp(peak - top)
            stat_ref[line, pl.ds(half, 1), :] = top
            stat_ref[line, pl.ds(2 + half, 1), :] = jnp.sum(sum_ref[at].T * rescale, axis=0, keepdims=True)
            stat_ref[line, pl.ds(4 + half, 1), :] = jnp.sum(dot_ref[at].T * rescale, axis=0, keepdims=True)
            stat_ref[line, pl.ds(6 + half, 1), :] = jnp.sum(pick_ref[at].T, axis=0, keepdims=True)
        every_ref[mine, line] = stat_ref[line]

    def spread(line):
        @pl.loop(1, SIDE * SIDE)
        def _(step):
            peer = lax.rem(mine + step, SIDE * SIDE)
            pltpu.make_async_remote_copy(
                src_ref=stat_ref.at[line], dst_ref=every_ref.at[mine, line], send_sem=stat_send.at[0], recv_sem=stat_recv.at[0],
                device_id=(tok, shard_of(peer // SIDE, lax.rem(peer, SIDE))), device_id_type=MESH,
            ).start()

    def spread_tok(ref, index, send_sem, recv_sem):
        copies = []
        for step in range(1, n_tok):
            copy = pltpu.make_async_remote_copy(
                src_ref=ref.at[index], dst_ref=ref.at[index], send_sem=send_sem.at[step], recv_sem=recv_sem.at[step],
                device_id=(lax.rem(tok + step, n_tok), voc), device_id_type=MESH,
            )
            copy.start()
            copies.append(copy)
        return copies

    def steps(position, first):
        line = lines[position]
        one, two = buffers[first], buffers[1 - first]

        @pl.loop(0, (chunks - 1) // 2)
        def _(pair):
            multiply(line, 2 * pair + 1, two)
            collect(2 * pair, one)
            multiply(line, 2 * pair + 2, one)
            collect(2 * pair + 1, two)

    for copy in weight_copies:
        copy.wait()
    begin(lines[0])
    multiply(lines[0], 0, buffers[0])
    for position in range(4):
        first = position % 2
        steps(position, first)
        if position == 0:
            for k, a_at in enumerate((a, a_prev, a_next, a_far)):
                landed(rows_ref, rows_at(b_prev, a_at, whole), row_sems, 4 + 2 * k)
                landed(rows_ref, rows_at(b_next, a_at, whole), row_sems, 5 + 2 * k)
            sends.append(send(rows_ref, (b_prev, slice(None), left), row_sems, 12, to_b_next))
            sends.append(send(rows_ref, (b_next, slice(None), right), row_sems, 13, to_b_prev))
            landed(meta_ref, (b_prev,), meta_sems, 3)
            landed(meta_ref, (b_next,), meta_sems, 4)
            sends.append(send(meta_ref, (b_prev,), meta_sems, 5, to_b_next))
        if position == 2:
            landed(rows_ref, (b_far, slice(None), left), row_sems, 12)
            landed(rows_ref, (b_far, slice(None), right), row_sems, 13)
            landed(meta_ref, (b_far,), meta_sems, 5)
        if position < 3:
            multiply(lines[position + 1], 0, buffers[1 - first])
        collect(chunks - 1, buffers[first])
        finish(lines[position])
        if position < 3:
            begin(lines[position + 1])
        if position == 2:
            for line in lines[:3]:
                spread(line)
            for line in range(SIDE):
                for half in range(2):
                    both = meta_ref[line, 2 * half] + meta_ref[line, 2 * half + 1]
                    code_ref[pl.ds(2 * line + half, 1), :] = both[1:2]
                    owner_ref[tok, pl.ds(2 * line + half, 1), :] = both[2:3]
            owner_copies = spread_tok(owner_ref, (tok,), owner_send, owner_recv)
    spread(lines[3])
    for copy in sends:
        copy.wait_send()
    for copy in owner_copies:
        copy.wait()
    others = every_ref.at[pl.ds(0, SIDE * SIDE - 1)]
    pltpu.make_async_copy(others, others, stat_recv.at[0]).wait()
    pltpu.make_async_copy(others, others, stat_send.at[0]).wait()

    peers = range(SIDE * SIDE)
    for line in range(SIDE):
        peaks = [every_ref[s, line, pl.ds(0, 2), :] for s in peers]
        top = functools.reduce(jnp.maximum, peaks)
        exp_sum = exp_dot = picked = jnp.zeros((2, 128), jnp.float32)
        for s in peers:
            rescale = jnp.exp(peaks[s] - top)
            exp_sum = exp_sum + every_ref[s, line, pl.ds(2, 2), :] * rescale
            exp_dot = exp_dot + every_ref[s, line, pl.ds(4, 2), :] * rescale
            picked = picked + every_ref[s, line, pl.ds(6, 2), :]
        log_total = jnp.log(exp_sum)
        final_ref[tok, 0, pl.ds(2 * line, 2), :] = picked - top - log_total
        final_ref[tok, 1, pl.ds(2 * line, 2), :] = top + log_total - exp_dot / exp_sum
    code = code_ref[...].astype(jnp.int32)
    shift = jnp.where(code > 0, lax.broadcasted_iota(jnp.int32, (8, 128), 1) + 1 - code, -1)
    for kind in range(2):
        score = final_ref[tok, kind]
        placed = jnp.zeros((8, 128), jnp.float32)
        for amount in range(span - LIVE + 1):
            moved = score if amount == 0 else pltpu.roll(score, amount, 1)
            placed = jnp.where(shift == amount, moved, placed)
        final_ref[tok, kind] = placed
    for copy in spread_tok(final_ref, (tok,), final_send, final_recv):
        copy.wait()
    for k in range(req_dev):
        wanted = ((tok * SIDE * SIDE + voc) * req_dev + k).astype(jnp.float32)
        for kind, out_ref in enumerate((logprob_ref, entropy_ref)):
            found = jnp.zeros((8, 128), jnp.float32)
            for t in range(n_tok):
                found = found + jnp.where(owner_ref[t] == wanted, final_ref[t, kind], 0.0)
            found = jnp.sum(found, axis=0, keepdims=True)
            out_ref[pl.ds(k, 1), :] = sum(found[:, part * span:(part + 1) * span] for part in range(128 // span))


def shards(n_tok, columns, hidden, norm_gain, head_weight, lengths, offsets, slot_request, targets):
    req_dev, span, width = hidden.shape
    vocab_dev = head_weight.shape[1]
    chunks = vocab_dev // columns
    line_rows = SIDE * req_dev * LIVE
    f32 = jnp.float32
    vmem, smem = pl.BlockSpec(memory_space=pltpu.VMEM), pl.BlockSpec(memory_space=pltpu.SMEM)
    dma = pltpu.SemaphoreType.DMA
    return pl.pallas_call(
        functools.partial(kernel, n_tok, columns),
        out_shape=(jax.ShapeDtypeStruct((req_dev, span), f32),) * 2,
        in_specs=[vmem, vmem, vmem, smem, smem, smem, pl.BlockSpec(memory_space=pl.ANY)],
        out_specs=(vmem, vmem),
        scratch_shapes=[
            pltpu.VMEM((req_dev * span, width), jnp.bfloat16),
            pltpu.VMEM((SIDE, line_rows, width), jnp.bfloat16),
            pltpu.VMEM((SIDE, SIDE, 8, 128), f32),
            pltpu.VMEM((chunks, width, columns), jnp.bfloat16),
            pltpu.VMEM((line_rows, columns), f32),
            pltpu.VMEM((line_rows, columns), f32),
            pltpu.VMEM((256, 128), f32),
            pltpu.VMEM((256, 128), f32),
            pltpu.VMEM((256, 128), f32),
            pltpu.VMEM((256, 128), f32),
            pltpu.VMEM((256, 128), jnp.int32),
            pltpu.VMEM((SIDE, 8, 128), f32),
            pltpu.VMEM((SIDE * SIDE, SIDE, 8, 128), f32),
            pltpu.VMEM((8, 128), f32),
            pltpu.VMEM((n_tok, 2, 8, 128), f32),
            pltpu.VMEM((n_tok, 8, 128), f32),
            dma((chunks,)),
            dma((14,)), dma((14,)), dma((6,)), dma((6,)),
            dma((1,)), dma((1,)), dma((n_tok,)), dma((n_tok,)), dma((n_tok,)), dma((n_tok,)),
        ],
        compiler_params=pltpu.CompilerParams(
            collective_id=0, has_side_effects=True, vmem_limit_bytes=58 * 2**20
        ),
        name="score",
    )(hidden, norm_gain.reshape(1, width), targets, lengths, offsets, slot_request, head_weight)


def solution(mesh, columns=1280):
    placed = (
        P(("tok", "voc"), None, None),
        P(),
        P(None, "voc"),
        P(("tok", "voc")),
        P(("tok", "voc")),
        P(),
        P(("tok", "voc"), None),
    )
    return jax.shard_map(
        functools.partial(shards, mesh.shape["tok"], columns),
        mesh=mesh,
        in_specs=placed,
        out_specs=(P(("tok", "voc"), None), P(("tok", "voc"), None)),
        check_vma=False,
    )
```

```python
import functools

import jax
import jax.numpy as jnp
from jax import lax
from jax.experimental import pallas as pl
from jax.experimental.pallas import tpu as pltpu
from jax.sharding import PartitionSpec as P

EPS = 1e-06
LIVE = 24
SIDE = 4
LOW = -1e30
MESH = pl.DeviceIdType.MESH


def kernel(
    n_tok, columns,
    hidden_ref, gain_ref, targets_ref, lengths_ref, offsets_ref, request_ref, weight_hbm,
    out_ref,
    normed_ref, rows_ref, meta_ref, weight_ref, even_ref, odd_ref,
    peak_ref, sum_ref, dot_ref, pick_ref, goal_ref,
    stat_ref, every_ref, code_ref, final_ref, owner_ref,
    weight_sem, row_send, row_recv, meta_send, meta_recv,
    stat_send, stat_recv, owner_send, owner_recv, final_send, final_recv,
):
    req_dev, span, width = hidden_ref.shape
    vocab_dev = weight_hbm.shape[1]
    chunks = vocab_dev // columns
    shard_rows = req_dev * LIVE
    tok, voc = lax.axis_index("tok"), lax.axis_index("voc")
    core = lax.rem(tok, 2)
    high, low = voc // SIDE, lax.rem(voc, SIDE)
    a = low + core * (high - low)
    b = high + core * (low - high)

    def shard_of(b_at, a_at):
        high_at = b_at + core * (a_at - b_at)
        low_at = a_at + core * (b_at - a_at)
        return high_at * SIDE + low_at

    def ring(place, step):
        return lax.rem(place + step + SIDE, SIDE)

    a_next, a_prev, a_far = ring(a, 1), ring(a, -1), ring(a, 2)
    b_next, b_prev, b_far = ring(b, 1), ring(b, -1), ring(b, 2)
    mine = b * SIDE + a

    weight_copies = [
        pltpu.make_async_copy(weight_hbm.at[:, pl.ds(c * columns, columns)], weight_ref.at[c], weight_sem.at[c])
        for c in range(chunks)
    ]
    for copy in weight_copies:
        copy.start()

    barrier = pltpu.get_barrier_semaphore()
    to_a_next, to_a_prev = (tok, shard_of(b, a_next)), (tok, shard_of(b, a_prev))
    to_b_next, to_b_prev = (tok, shard_of(b_next, a)), (tok, shard_of(b_prev, a))
    for peer in (to_a_next, to_a_prev, to_b_next, to_b_prev):
        pl.semaphore_signal(barrier, inc=1, device_id=peer, device_id_type=MESH)
    for step in range(1, n_tok):
        pl.semaphore_signal(barrier, inc=1, device_id=(lax.rem(tok + step, n_tok), voc), device_id_type=MESH)

    lane = lax.broadcasted_iota(jnp.int32, (1, 128), 1)
    which = lax.rem(lane // span, req_dev)
    own_half = lane // (req_dev * span) == lax.rem(a, 2)
    offset = jnp.where(which == 0, offsets_ref[0], offsets_ref[1])
    length = jnp.where(which == 0, lengths_ref[0], lengths_ref[1])
    relative = lax.rem(lane, span) - offset
    alive = own_half & (relative >= 0) & (relative < length)
    code = jnp.where(alive, (lane // span) * span + relative + 1, 0)
    first_slot = (tok * SIDE * SIDE + voc) * req_dev
    request = jnp.where(own_half, jnp.where(which == 0, request_ref[first_slot], request_ref[first_slot + 1]), 0)
    goals = targets_ref[...]
    goals = jnp.concatenate([goals[0:1], goals[1:2], goals[0:1], goals[1:2]], axis=1)
    goals = jnp.where(own_half, goals, 0)
    meta_ref[b, a] = jnp.concatenate(
        [goals.astype(jnp.float32), code.astype(jnp.float32), request.astype(jnp.float32), jnp.zeros((5, 128), jnp.float32)], axis=0
    )

    for j in range(req_dev):
        values = hidden_ref[j].astype(jnp.float32)
        square = jnp.mean(values * values, axis=-1, keepdims=True)
        normed_ref[pl.ds(j * span, span), :] = (values * lax.rsqrt(square + EPS) * gain_ref[...]).astype(jnp.bfloat16)
    row = lax.broadcasted_iota(jnp.int32, (shard_rows, req_dev * span), 0)
    column = lax.broadcasted_iota(jnp.int32, (shard_rows, req_dev * span), 1)
    source = jnp.where(row < LIVE, row + offsets_ref[0], row - LIVE + span + offsets_ref[1])
    chosen = jnp.where(source == column, 1.0, 0.0).astype(jnp.bfloat16)
    rows_ref[pl.ds(0, shard_rows), :] = jnp.dot(
        chosen, normed_ref[...], preferred_element_type=jnp.float32
    ).astype(jnp.bfloat16)
    peak_ref[...] = jnp.full_like(peak_ref, LOW)
    sum_ref[...] = jnp.zeros_like(sum_ref)
    dot_ref[...] = jnp.zeros_like(dot_ref)
    pick_ref[...] = jnp.zeros_like(pick_ref)

    line_rows = SIDE * shard_rows
    sub_row = lax.broadcasted_iota(jnp.int32, (128, 128), 0).astype(jnp.float32) + 1.0
    sub_lane = lax.broadcasted_iota(jnp.int32, (128, 128), 1)
    lines = (b, b_next, b_prev, b_far)
    a_order = (a, a_next, a_far, a_prev)
    buffers = (even_ref, odd_ref)
    blocks = ((0, shard_rows), (shard_rows, 3 * shard_rows), (line_rows, 2 * line_rows), (3 * line_rows, line_rows))
    sends = []

    def push(ref, source, target, sems, place, peer):
        copy = pltpu.make_async_remote_copy(
            src_ref=ref.at[source], dst_ref=ref.at[target], send_sem=sems[0].at[place], recv_sem=sems[1].at[place],
            device_id=peer, device_id_type=MESH,
        )
        copy.start()
        sends.append(copy)
        return copy

    def landed(ref, index, sems, place):
        pltpu.make_async_copy(ref.at[index], ref.at[index], sems[1].at[place]).wait()

    row_sems, meta_sems = (row_send, row_recv), (meta_send, meta_recv)
    whole, left, right = pl.ds(0, width), pl.ds(0, width // 2), pl.ds(width // 2, width // 2)

    def shard(line, place, part=whole):
        return (pl.ds(line * line_rows + place * shard_rows, shard_rows), part)

    def whole_line(line, part):
        return (pl.ds(line * line_rows, line_rows), part)

    def goals_of(position):
        line = lines[position]
        for half in range(2):
            both = meta_ref[line, 2 * half] + meta_ref[line, 2 * half + 1]
            goal = jnp.sum(jnp.where(both[1:2] == sub_row, both[0:1], 0.0), axis=1, keepdims=True)
            at = pl.ds(position * 256 + half * 128, 128)
            goal_ref[at, :] = goal.astype(jnp.int32) - voc * vocab_dev - sub_lane

    def own_goals():
        both = meta_ref[b, a]
        for half in range(2):
            goal = jnp.sum(jnp.where(both[1:2] == sub_row, both[0:1], 0.0), axis=1, keepdims=True)
            goal_ref[pl.ds(half * 128, 128), :] = goal.astype(jnp.int32) - voc * vocab_dev - sub_lane

    def multiply(block, chunk, buffer):
        start, count = blocks[block]
        buffer[pl.ds(0, count), :] = jnp.dot(
            rows_ref[pl.ds(start, count), :], weight_ref[chunk], preferred_element_type=jnp.float32
        )

    def collect(block, chunk, buffer):
        start, count = blocks[block]
        for group in range(count // 8):
            flat = start + group * 8
            position, place = flat // line_rows, flat % line_rows // shard_rows
            request_at, part = flat % shard_rows // LIVE, flat % LIVE
            base = position * 256 + request_at * span + part
            at = pl.ds(pl.multiple_of(a_order[place] * (req_dev * span) + base, 8), 8)
            logits = [buffer[pl.ds(group * 8, 8), pl.ds(c * 128, 128)] for c in range(columns // 128)]
            peak = peak_ref[at]
            top = functools.reduce(jnp.maximum, logits, peak)
            rescale = jnp.exp(peak - top)
            exp_sum, exp_dot = sum_ref[at] * rescale, dot_ref[at] * rescale
            picked, goal = pick_ref[at], goal_ref[at]
            for c, logit in enumerate(logits):
                scaled = jnp.exp(logit - top)
                exp_sum = exp_sum + scaled
                exp_dot = exp_dot + scaled * logit
                picked = jnp.where(goal == chunk * columns + c * 128, logit, picked)
            peak_ref[at], sum_ref[at], dot_ref[at], pick_ref[at] = top, exp_sum, exp_dot, picked

    def finish(position):
        for half in range(2):
            at = pl.ds(position * 256 + half * 128, 128)
            peak = peak_ref[at].T
            top = jnp.max(peak, axis=0, keepdims=True)
            rescale = jnp.exp(peak - top)
            stat_ref[position, pl.ds(half, 1), :] = top
            stat_ref[position, pl.ds(2 + half, 1), :] = jnp.sum(sum_ref[at].T * rescale, axis=0, keepdims=True)
            stat_ref[position, pl.ds(4 + half, 1), :] = jnp.sum(dot_ref[at].T * rescale, axis=0, keepdims=True)
            stat_ref[position, pl.ds(6 + half, 1), :] = jnp.sum(pick_ref[at].T, axis=0, keepdims=True)

    far_first = sorted(
        ((i, j) for i in range(SIDE) for j in range(SIDE) if i or j), key=lambda s: -(min(s[0], SIDE - s[0]) + min(s[1], SIDE - s[1]))
    )

    def spread(position):
        for i, j in far_first:
            pltpu.make_async_remote_copy(
                src_ref=stat_ref.at[position], dst_ref=every_ref.at[mine, lines[position]],
                send_sem=stat_send.at[0], recv_sem=stat_recv.at[0],
                device_id=(tok, shard_of(ring(b, i), ring(a, j))), device_id_type=MESH,
            ).start()
        every_ref[mine, lines[position]] = stat_ref[position]

    def spread_tok(ref, index, send_sem, recv_sem):
        copies = []
        for step in sorted(range(1, n_tok), key=lambda k: -min(k, n_tok - k)):
            copy = pltpu.make_async_remote_copy(
                src_ref=ref.at[index], dst_ref=ref.at[index], send_sem=send_sem.at[step], recv_sem=recv_sem.at[step],
                device_id=(lax.rem(tok + step, n_tok), voc), device_id_type=MESH,
            )
            copy.start()
            copies.append(copy)
        return copies

    def steps(block, first):
        one, two = buffers[first], buffers[1 - first]

        @pl.loop(0, (chunks - 1) // 2)
        def _(pair):
            multiply(block, 2 * pair + 1, two)
            collect(block, 2 * pair, one)
            multiply(block, 2 * pair + 2, one)
            collect(block, 2 * pair + 1, two)

    pl.semaphore_wait(barrier, 4 + n_tok - 1)
    own_next = push(rows_ref, shard(0, 0), shard(0, 3), row_sems, 0, to_a_next)
    own_prev = push(rows_ref, shard(0, 0), shard(0, 1), row_sems, 1, to_a_prev)
    push(meta_ref, (b, a), (b, a), meta_sems, 0, to_a_next)
    push(meta_ref, (b, a), (b, a), meta_sems, 1, to_a_prev)
    own_goals()

    for chunk in range(chunks):
        weight_copies[chunk].wait()
        multiply(0, chunk, buffers[chunk % 2])
        if chunk > 0:
            collect(0, chunk - 1, buffers[1 - chunk % 2])
        if chunk == min(1, chunks - 1):
            own_next.wait_send()
            own_prev.wait_send()
            push(rows_ref, shard(0, 0), shard(2, 0), row_sems, 4, to_b_next)
            push(rows_ref, shard(0, 0), shard(1, 0), row_sems, 5, to_b_prev)
        if chunk == min(2, chunks - 1):
            landed(rows_ref, shard(0, 3), row_sems, 0)
            push(rows_ref, shard(0, 3, left), shard(0, 2, left), row_sems, 2, to_a_next)
            landed(rows_ref, shard(0, 1), row_sems, 1)
            push(rows_ref, shard(0, 1, right), shard(0, 2, right), row_sems, 3, to_a_prev)
            landed(meta_ref, (b, a_prev), meta_sems, 0)
            push(meta_ref, (b, a_prev), (b, a_prev), meta_sems, 2, to_a_next)
            landed(meta_ref, (b, a_next), meta_sems, 1)
            for k, place in enumerate((1, 3)):
                push(rows_ref, shard(0, place), shard(2, place), row_sems, 6 + 2 * k, to_b_next)
                push(rows_ref, shard(0, place), shard(1, place), row_sems, 7 + 2 * k, to_b_prev)
    landed(rows_ref, shard(0, 2, left), row_sems, 2)
    landed(rows_ref, shard(0, 2, right), row_sems, 3)
    push(rows_ref, shard(0, 2), shard(2, 2), row_sems, 10, to_b_next)
    push(rows_ref, shard(0, 2), shard(1, 2), row_sems, 11, to_b_prev)
    landed(meta_ref, (b, a_far), meta_sems, 2)
    push(meta_ref, (b,), (b,), meta_sems, 3, to_b_next)
    push(meta_ref, (b,), (b,), meta_sems, 4, to_b_prev)

    at_chunk = (chunks - 1) % 2
    multiply(1, 0, buffers[1 - at_chunk])
    collect(0, chunks - 1, buffers[at_chunk])
    goals_of(0)
    first = 1 - at_chunk
    steps(1, first)
    for k, place in enumerate((0, 1, 3, 2)):
        landed(rows_ref, shard(2, place), row_sems, 4 + 2 * k)
        landed(rows_ref, shard(1, place), row_sems, 5 + 2 * k)
    push(rows_ref, whole_line(2, left), whole_line(3, left), row_sems, 12, to_b_next)
    push(rows_ref, whole_line(1, right), whole_line(3, right), row_sems, 13, to_b_prev)
    landed(meta_ref, (b_prev,), meta_sems, 3)
    landed(meta_ref, (b_next,), meta_sems, 4)
    push(meta_ref, (b_prev,), (b_prev,), meta_sems, 5, to_b_next)
    multiply(2, 0, buffers[1 - first])
    collect(1, chunks - 1, buffers[first])
    finish(0)
    goals_of(1)
    goals_of(2)
    first = 1 - first
    steps(2, first)
    landed(rows_ref, whole_line(3, left), row_sems, 12)
    landed(rows_ref, whole_line(3, right), row_sems, 13)
    landed(meta_ref, (b_far,), meta_sems, 5)
    multiply(3, 0, buffers[1 - first])
    collect(2, chunks - 1, buffers[first])
    goals_of(3)
    finish(1)
    finish(2)
    for position in range(3):
        spread(position)
    for line in range(SIDE):
        for half in range(2):
            both = meta_ref[line, 2 * half] + meta_ref[line, 2 * half + 1]
            code_ref[pl.ds(2 * line + half, 1), :] = both[1:2]
            owner_ref[tok, pl.ds(2 * line + half, 1), :] = both[2:3]
    owner_copies = spread_tok(owner_ref, (tok,), owner_send, owner_recv)
    first = 1 - first
    steps(3, first)
    collect(3, chunks - 1, buffers[first])
    finish(3)
    spread(3)
    for copy in sends:
        if copy is not own_next and copy is not own_prev:
            copy.wait_send()
    for copy in owner_copies:
        copy.wait()
    others = every_ref.at[pl.ds(0, SIDE * SIDE - 1)]
    pltpu.make_async_copy(others, others, stat_recv.at[0]).wait()
    pltpu.make_async_copy(others, others, stat_send.at[0]).wait()

    peers = range(SIDE * SIDE)
    for line in range(SIDE):
        peaks = [every_ref[s, line, pl.ds(0, 2), :] for s in peers]
        top = functools.reduce(jnp.maximum, peaks)
        exp_sum = exp_dot = picked = jnp.zeros((2, 128), jnp.float32)
        for s in peers:
            rescale = jnp.exp(peaks[s] - top)
            exp_sum = exp_sum + every_ref[s, line, pl.ds(2, 2), :] * rescale
            exp_dot = exp_dot + every_ref[s, line, pl.ds(4, 2), :] * rescale
            picked = picked + every_ref[s, line, pl.ds(6, 2), :]
        log_total = jnp.log(exp_sum)
        final_ref[tok, 0, pl.ds(2 * line, 2), :] = picked - top - log_total
        final_ref[tok, 1, pl.ds(2 * line, 2), :] = top + log_total - exp_dot / exp_sum
    code = code_ref[...].astype(jnp.int32)
    shift = jnp.where(code > 0, lax.broadcasted_iota(jnp.int32, (8, 128), 1) + 1 - code, -1)
    for kind in range(2):
        score = final_ref[tok, kind]
        placed = jnp.zeros((8, 128), jnp.float32)
        for amount in range(span - LIVE + 1):
            moved = score if amount == 0 else pltpu.roll(score, amount, 1)
            placed = jnp.where(shift == amount, moved, placed)
        final_ref[tok, kind] = placed
    for copy in spread_tok(final_ref, (tok,), final_send, final_recv):
        copy.wait()
    for k in range(req_dev):
        wanted = ((tok * SIDE * SIDE + voc) * req_dev + k).astype(jnp.float32)
        for kind in range(2):
            found = jnp.zeros((8, 128), jnp.float32)
            for t in range(n_tok):
                found = found + jnp.where(owner_ref[t] == wanted, final_ref[t, kind], 0.0)
            found = jnp.sum(found, axis=0, keepdims=True)
            out_ref[pl.ds(kind * req_dev + k, 1), :] = sum(found[:, part * span:(part + 1) * span] for part in range(128 // span))


def shards(n_tok, columns, hidden, norm_gain, head_weight, lengths, offsets, slot_request, targets):
    req_dev, span, width = hidden.shape
    vocab_dev = head_weight.shape[1]
    chunks = vocab_dev // columns
    line_rows = SIDE * req_dev * LIVE
    f32 = jnp.float32
    vmem, smem = pl.BlockSpec(memory_space=pltpu.VMEM), pl.BlockSpec(memory_space=pltpu.SMEM)
    dma = pltpu.SemaphoreType.DMA
    scores = pl.pallas_call(
        functools.partial(kernel, n_tok, columns),
        out_shape=jax.ShapeDtypeStruct((2 * req_dev, span), f32),
        in_specs=[vmem, vmem, vmem, smem, smem, smem, pl.BlockSpec(memory_space=pl.ANY)],
        out_specs=vmem,
        scratch_shapes=[
            pltpu.VMEM((req_dev * span, width), jnp.bfloat16),
            pltpu.VMEM((SIDE * line_rows, width), jnp.bfloat16),
            pltpu.VMEM((SIDE, SIDE, 8, 128), f32),
            pltpu.VMEM((chunks, width, columns), jnp.bfloat16),
            pltpu.VMEM((2 * line_rows, columns), f32),
            pltpu.VMEM((2 * line_rows, columns), f32),
            pltpu.VMEM((SIDE * 256, 128), f32),
            pltpu.VMEM((SIDE * 256, 128), f32),
            pltpu.VMEM((SIDE * 256, 128), f32),
            pltpu.VMEM((SIDE * 256, 128), f32),
            pltpu.VMEM((SIDE * 256, 128), jnp.int32),
            pltpu.VMEM((SIDE, 8, 128), f32),
            pltpu.VMEM((SIDE * SIDE, SIDE, 8, 128), f32),
            pltpu.VMEM((8, 128), f32),
            pltpu.VMEM((n_tok, 2, 8, 128), f32),
            pltpu.VMEM((n_tok, 8, 128), f32),
            dma((chunks,)),
            dma((14,)), dma((14,)), dma((6,)), dma((6,)),
            dma((1,)), dma((1,)), dma((n_tok,)), dma((n_tok,)), dma((n_tok,)), dma((n_tok,)),
        ],
        compiler_params=pltpu.CompilerParams(
            collective_id=0, has_side_effects=True, vmem_limit_bytes=58 * 2**20
        ),
        name="score",
    )(hidden, norm_gain.reshape(1, width), targets, lengths, offsets, slot_request, head_weight)
    return scores[:req_dev], scores[req_dev:]


def solution(mesh, columns=1280):
    placed = (
        P(("tok", "voc"), None, None),
        P(),
        P(None, "voc"),
        P(("tok", "voc")),
        P(("tok", "voc")),
        P(),
        P(("tok", "voc"), None),
    )
    return jax.shard_map(
        functools.partial(shards, mesh.shape["tok"], columns),
        mesh=mesh,
        in_specs=placed,
        out_specs=(P(("tok", "voc"), None), P(("tok", "voc"), None)),
        check_vma=False,
    )
```

```python
import functools

import jax
import jax.numpy as jnp
from jax import lax
from jax.experimental import pallas as pl
from jax.experimental.pallas import tpu as pltpu
from jax.sharding import PartitionSpec as P

EPS = 1e-06
LIVE = 24
SIDE = 4
LOW = -1e30
MESH = pl.DeviceIdType.MESH


def kernel(
    n_tok, columns,
    hidden_hbm, gain_hbm, targets_hbm, lengths_hbm, offsets_hbm, request_hbm, weight_hbm,
    out_ref,
    hidden_ref, gain_ref, targets_ref, lengths_ref, offsets_ref, request_ref, input_sem,
    normed_ref, rows_ref, meta_ref, weight_ref, even_ref, odd_ref,
    peak_ref, sum_ref, dot_ref, pick_ref, goal_ref,
    stat_ref, every_ref, code_ref, final_ref, owner_ref,
    weight_sem, row_send, row_recv, meta_send, meta_recv,
    stat_send, stat_recv, owner_send, owner_recv, final_send, final_recv,
):
    req_dev, span, width = hidden_hbm.shape
    vocab_dev = weight_hbm.shape[1]
    chunks = vocab_dev // columns
    shard_rows = req_dev * LIVE
    tok, voc = lax.axis_index("tok"), lax.axis_index("voc")
    core = lax.rem(tok, 2)
    high, low = voc // SIDE, lax.rem(voc, SIDE)
    a = low + core * (high - low)
    b = high + core * (low - high)

    def shard_of(b_at, a_at):
        high_at = b_at + core * (a_at - b_at)
        low_at = a_at + core * (b_at - a_at)
        return high_at * SIDE + low_at

    def ring(place, step):
        return lax.rem(place + step + SIDE, SIDE)

    a_next, a_prev, a_far = ring(a, 1), ring(a, -1), ring(a, 2)
    b_next, b_prev, b_far = ring(b, 1), ring(b, -1), ring(b, 2)
    mine = b * SIDE + a

    pairs = (
        (hidden_hbm, hidden_ref), (gain_hbm, gain_ref), (targets_hbm, targets_ref),
        (lengths_hbm, lengths_ref), (offsets_hbm, offsets_ref), (request_hbm, request_ref),
    )
    inputs = [pltpu.make_async_copy(src, dst, input_sem.at[n]) for n, (src, dst) in enumerate(pairs)]
    for copy in inputs:
        copy.start()

    barrier = pltpu.get_barrier_semaphore()
    to_a_next, to_a_prev = (tok, shard_of(b, a_next)), (tok, shard_of(b, a_prev))
    to_b_next, to_b_prev = (tok, shard_of(b_next, a)), (tok, shard_of(b_prev, a))
    for peer in (to_a_next, to_a_prev, to_b_next, to_b_prev):
        pl.semaphore_signal(barrier, inc=1, device_id=peer, device_id_type=MESH)
    for step in range(1, n_tok):
        pl.semaphore_signal(barrier, inc=1, device_id=(lax.rem(tok + step, n_tok), voc), device_id_type=MESH)

    weight_copies = [
        pltpu.make_async_copy(weight_hbm.at[:, pl.ds(c * columns, columns)], weight_ref.at[c], weight_sem.at[c])
        for c in range(chunks)
    ]
    for copy in weight_copies:
        copy.start()

    for copy in inputs:
        copy.wait()

    lane = lax.broadcasted_iota(jnp.int32, (1, 128), 1)
    which = lax.rem(lane // span, req_dev)
    own_half = lane // (req_dev * span) == lax.rem(a, 2)
    offset = jnp.where(which == 0, offsets_ref[0], offsets_ref[1])
    length = jnp.where(which == 0, lengths_ref[0], lengths_ref[1])
    relative = lax.rem(lane, span) - offset
    alive = own_half & (relative >= 0) & (relative < length)
    code = jnp.where(alive, (lane // span) * span + relative + 1, 0)
    first_slot = (tok * SIDE * SIDE + voc) * req_dev
    request = jnp.where(own_half, jnp.where(which == 0, request_ref[first_slot], request_ref[first_slot + 1]), 0)
    goals = targets_ref[...]
    goals = jnp.concatenate([goals[0:1], goals[1:2], goals[0:1], goals[1:2]], axis=1)
    goals = jnp.where(own_half, goals, 0)
    meta_ref[b, a] = jnp.concatenate(
        [goals.astype(jnp.float32), code.astype(jnp.float32), request.astype(jnp.float32), jnp.zeros((5, 128), jnp.float32)], axis=0
    )

    for j in range(req_dev):
        values = hidden_ref[j].astype(jnp.float32)
        square = jnp.mean(values * values, axis=-1, keepdims=True)
        normed_ref[pl.ds(j * span, span), :] = (values * lax.rsqrt(square + EPS) * gain_ref[...]).astype(jnp.bfloat16)
    row = lax.broadcasted_iota(jnp.int32, (shard_rows, req_dev * span), 0)
    column = lax.broadcasted_iota(jnp.int32, (shard_rows, req_dev * span), 1)
    source = jnp.where(row < LIVE, row + offsets_ref[0], row - LIVE + span + offsets_ref[1])
    chosen = jnp.where(source == column, 1.0, 0.0).astype(jnp.bfloat16)
    rows_ref[pl.ds(0, shard_rows), :] = jnp.dot(
        chosen, normed_ref[...], preferred_element_type=jnp.float32
    ).astype(jnp.bfloat16)
    peak_ref[...] = jnp.full_like(peak_ref, LOW)
    sum_ref[...] = jnp.zeros_like(sum_ref)
    dot_ref[...] = jnp.zeros_like(dot_ref)
    pick_ref[...] = jnp.zeros_like(pick_ref)

    line_rows = SIDE * shard_rows
    sub_row = lax.broadcasted_iota(jnp.int32, (128, 128), 0).astype(jnp.float32) + 1.0
    sub_lane = lax.broadcasted_iota(jnp.int32, (128, 128), 1)
    lines = (b, b_next, b_prev, b_far)
    a_order = (a, a_next, a_far, a_prev)
    buffers = (even_ref, odd_ref)
    order = (
        (0, 0), (0, 1), (0, 2), (0, 3), (1, 0), (1, 1), (2, 0), (2, 1),
        (1, 3), (1, 2), (2, 3), (2, 2), (3, 0), (3, 1), (3, 3), (3, 2),
    )
    blocks = tuple((at * shard_rows, n * shard_rows) for at, n in ((0, 1), (1, 3), (4, 4), (8, 4), (12, 4)))
    sends = []

    def push(ref, source, target, sems, place, peer):
        copy = pltpu.make_async_remote_copy(
            src_ref=ref.at[source], dst_ref=ref.at[target], send_sem=sems[0].at[place], recv_sem=sems[1].at[place],
            device_id=peer, device_id_type=MESH,
        )
        copy.start()
        sends.append(copy)
        return copy

    def landed(ref, index, sems, place):
        pltpu.make_async_copy(ref.at[index], ref.at[index], sems[1].at[place]).wait()

    row_sems, meta_sems = (row_send, row_recv), (meta_send, meta_recv)
    whole, left, right = pl.ds(0, width), pl.ds(0, width // 2), pl.ds(width // 2, width // 2)

    def shard(line, place, part=whole):
        return (pl.ds(order.index((line, place)) * shard_rows, shard_rows), part)

    def couple(first, part):
        return (pl.ds(first * shard_rows, 2 * shard_rows), part)

    def goals_of(position):
        line = lines[position]
        for half in range(2):
            both = meta_ref[line, 2 * half] + meta_ref[line, 2 * half + 1]
            goal = jnp.sum(jnp.where(both[1:2] == sub_row, both[0:1], 0.0), axis=1, keepdims=True)
            at = pl.ds(position * 256 + half * 128, 128)
            goal_ref[at, :] = goal.astype(jnp.int32) - voc * vocab_dev - sub_lane

    def own_goals():
        both = meta_ref[b, a]
        for half in range(2):
            goal = jnp.sum(jnp.where(both[1:2] == sub_row, both[0:1], 0.0), axis=1, keepdims=True)
            goal_ref[pl.ds(half * 128, 128), :] = goal.astype(jnp.int32) - voc * vocab_dev - sub_lane

    def multiply(block, chunk, buffer):
        start, count = blocks[block]
        buffer[pl.ds(0, count), :] = jnp.dot(
            rows_ref[pl.ds(start, count), :], weight_ref[chunk], preferred_element_type=jnp.float32
        )

    def collect(block, chunk, buffer):
        start, count = blocks[block]
        for group in range(count // 8):
            flat = start + group * 8
            position, place = order[flat // shard_rows]
            request_at, part = flat % shard_rows // LIVE, flat % LIVE
            base = position * 256 + request_at * span + part
            at = pl.ds(pl.multiple_of(a_order[place] * (req_dev * span) + base, 8), 8)
            logits = [buffer[pl.ds(group * 8, 8), pl.ds(c * 128, 128)] for c in range(columns // 128)]
            peak = peak_ref[at]
            top = functools.reduce(jnp.maximum, logits, peak)
            rescale = jnp.exp(peak - top)
            exp_sum, exp_dot = sum_ref[at] * rescale, dot_ref[at] * rescale
            picked, goal = pick_ref[at], goal_ref[at]
            for c, logit in enumerate(logits):
                scaled = jnp.exp(logit - top)
                exp_sum = exp_sum + scaled
                exp_dot = exp_dot + scaled * logit
                picked = jnp.where(goal == chunk * columns + c * 128, logit, picked)
            peak_ref[at], sum_ref[at], dot_ref[at], pick_ref[at] = top, exp_sum, exp_dot, picked

    def finish(position):
        for half in range(2):
            at = pl.ds(position * 256 + half * 128, 128)
            peak = peak_ref[at].T
            top = jnp.max(peak, axis=0, keepdims=True)
            rescale = jnp.exp(peak - top)
            stat_ref[position, pl.ds(half, 1), :] = top
            stat_ref[position, pl.ds(2 + half, 1), :] = jnp.sum(sum_ref[at].T * rescale, axis=0, keepdims=True)
            stat_ref[position, pl.ds(4 + half, 1), :] = jnp.sum(dot_ref[at].T * rescale, axis=0, keepdims=True)
            stat_ref[position, pl.ds(6 + half, 1), :] = jnp.sum(pick_ref[at].T, axis=0, keepdims=True)

    far_first = sorted(
        ((i, j) for i in range(SIDE) for j in range(SIDE) if i or j), key=lambda s: -(min(s[0], SIDE - s[0]) + min(s[1], SIDE - s[1]))
    )

    def spread(position):
        for i, j in far_first:
            pltpu.make_async_remote_copy(
                src_ref=stat_ref.at[position], dst_ref=every_ref.at[mine, lines[position]],
                send_sem=stat_send.at[0], recv_sem=stat_recv.at[0],
                device_id=(tok, shard_of(ring(b, i), ring(a, j))), device_id_type=MESH,
            ).start()
        every_ref[mine, lines[position]] = stat_ref[position]

    def spread_tok(ref, index, send_sem, recv_sem):
        copies = []
        for step in sorted(range(1, n_tok), key=lambda k: -min(k, n_tok - k)):
            copy = pltpu.make_async_remote_copy(
                src_ref=ref.at[index], dst_ref=ref.at[index], send_sem=send_sem.at[step], recv_sem=recv_sem.at[step],
                device_id=(lax.rem(tok + step, n_tok), voc), device_id_type=MESH,
            )
            copy.start()
            copies.append(copy)
        return copies

    def steps(block, first):
        one, two = buffers[first], buffers[1 - first]

        @pl.loop(0, (chunks - 1) // 2)
        def _(pair):
            multiply(block, 2 * pair + 1, two)
            collect(block, 2 * pair, one)
            multiply(block, 2 * pair + 2, one)
            collect(block, 2 * pair + 1, two)

    pl.semaphore_wait(barrier, 4 + n_tok - 1)
    own_next = push(rows_ref, shard(0, 0), shard(0, 3), row_sems, 0, to_a_next)
    own_prev = push(rows_ref, shard(0, 0), shard(0, 1), row_sems, 1, to_a_prev)
    push(meta_ref, (b, a), (b, a), meta_sems, 0, to_a_next)
    push(meta_ref, (b, a), (b, a), meta_sems, 1, to_a_prev)
    own_goals()

    for chunk in range(chunks):
        weight_copies[chunk].wait()
        multiply(0, chunk, buffers[chunk % 2])
        if chunk > 0:
            collect(0, chunk - 1, buffers[1 - chunk % 2])
        if chunk == min(1, chunks - 1):
            own_next.wait_send()
            own_prev.wait_send()
            push(rows_ref, shard(0, 0), shard(2, 0), row_sems, 4, to_b_next)
            push(rows_ref, shard(0, 0), shard(1, 0), row_sems, 5, to_b_prev)
        if chunk == min(2, chunks - 1):
            landed(rows_ref, shard(0, 3), row_sems, 0)
            push(rows_ref, shard(0, 3, left), shard(0, 2, left), row_sems, 2, to_a_next)
            landed(rows_ref, shard(0, 1), row_sems, 1)
            push(rows_ref, shard(0, 1, right), shard(0, 2, right), row_sems, 3, to_a_prev)
            landed(meta_ref, (b, a_prev), meta_sems, 0)
            push(meta_ref, (b, a_prev), (b, a_prev), meta_sems, 2, to_a_next)
            landed(meta_ref, (b, a_next), meta_sems, 1)
            for k, place in enumerate((1, 3)):
                push(rows_ref, shard(0, place), shard(2, place), row_sems, 6 + 2 * k, to_b_next)
                push(rows_ref, shard(0, place), shard(1, place), row_sems, 7 + 2 * k, to_b_prev)
    landed(rows_ref, shard(0, 2, left), row_sems, 2)
    landed(rows_ref, shard(0, 2, right), row_sems, 3)
    push(rows_ref, shard(0, 2), shard(2, 2), row_sems, 10, to_b_next)
    push(rows_ref, shard(0, 2), shard(1, 2), row_sems, 11, to_b_prev)
    landed(meta_ref, (b, a_far), meta_sems, 2)
    push(meta_ref, (b,), (b,), meta_sems, 3, to_b_next)
    push(meta_ref, (b,), (b,), meta_sems, 4, to_b_prev)

    at_chunk = (chunks - 1) % 2
    multiply(1, 0, buffers[1 - at_chunk])
    collect(0, chunks - 1, buffers[at_chunk])
    goals_of(0)
    first = 1 - at_chunk
    steps(1, first)
    for k, place in enumerate((0, 1)):
        landed(rows_ref, shard(2, place), row_sems, 4 + 2 * k)
        landed(rows_ref, shard(1, place), row_sems, 5 + 2 * k)
    push(rows_ref, couple(6, left), couple(12, left), row_sems, 12, to_b_next)
    push(rows_ref, couple(4, right), couple(12, right), row_sems, 13, to_b_prev)
    landed(meta_ref, (b_prev,), meta_sems, 3)
    landed(meta_ref, (b_next,), meta_sems, 4)
    push(meta_ref, (b_prev,), (b_prev,), meta_sems, 5, to_b_next)
    multiply(2, 0, buffers[1 - first])
    collect(1, chunks - 1, buffers[first])
    finish(0)
    goals_of(1)
    goals_of(2)
    first = 1 - first
    steps(2, first)
    for k, place in enumerate((3, 2)):
        landed(rows_ref, shard(2, place), row_sems, 8 + 2 * k)
        landed(rows_ref, shard(1, place), row_sems, 9 + 2 * k)
    push(rows_ref, couple(10, left), couple(14, left), row_sems, 14, to_b_next)
    push(rows_ref, couple(8, right), couple(14, right), row_sems, 15, to_b_prev)
    multiply(3, 0, buffers[1 - first])
    collect(2, chunks - 1, buffers[first])
    first = 1 - first
    steps(3, first)
    for k, at in enumerate((12, 14)):
        landed(rows_ref, couple(at, left), row_sems, 12 + 2 * k)
        landed(rows_ref, couple(at, right), row_sems, 13 + 2 * k)
    landed(meta_ref, (b_far,), meta_sems, 5)
    multiply(4, 0, buffers[1 - first])
    collect(3, chunks - 1, buffers[first])
    goals_of(3)
    finish(1)
    finish(2)
    for position in range(3):
        spread(position)
    for line in range(SIDE):
        for half in range(2):
            both = meta_ref[line, 2 * half] + meta_ref[line, 2 * half + 1]
            code_ref[pl.ds(2 * line + half, 1), :] = both[1:2]
            owner_ref[tok, pl.ds(2 * line + half, 1), :] = both[2:3]
    owner_copies = spread_tok(owner_ref, (tok,), owner_send, owner_recv)
    first = 1 - first
    steps(4, first)
    collect(4, chunks - 1, buffers[first])
    finish(3)
    spread(3)
    for copy in sends:
        if copy is not own_next and copy is not own_prev:
            copy.wait_send()
    for copy in owner_copies:
        copy.wait()
    others = every_ref.at[pl.ds(0, SIDE * SIDE - 1)]
    pltpu.make_async_copy(others, others, stat_recv.at[0]).wait()
    pltpu.make_async_copy(others, others, stat_send.at[0]).wait()

    peers = range(SIDE * SIDE)
    for line in range(SIDE):
        peaks = [every_ref[s, line, pl.ds(0, 2), :] for s in peers]
        top = functools.reduce(jnp.maximum, peaks)
        exp_sum = exp_dot = picked = jnp.zeros((2, 128), jnp.float32)
        for s in peers:
            rescale = jnp.exp(peaks[s] - top)
            exp_sum = exp_sum + every_ref[s, line, pl.ds(2, 2), :] * rescale
            exp_dot = exp_dot + every_ref[s, line, pl.ds(4, 2), :] * rescale
            picked = picked + every_ref[s, line, pl.ds(6, 2), :]
        log_total = jnp.log(exp_sum)
        final_ref[tok, 0, pl.ds(2 * line, 2), :] = picked - top - log_total
        final_ref[tok, 1, pl.ds(2 * line, 2), :] = top + log_total - exp_dot / exp_sum
    code = code_ref[...].astype(jnp.int32)
    shift = jnp.where(code > 0, lax.broadcasted_iota(jnp.int32, (8, 128), 1) + 1 - code, -1)
    for kind in range(2):
        score = final_ref[tok, kind]
        placed = jnp.zeros((8, 128), jnp.float32)
        for amount in range(span - LIVE + 1):
            moved = score if amount == 0 else pltpu.roll(score, amount, 1)
            placed = jnp.where(shift == amount, moved, placed)
        final_ref[tok, kind] = placed
    for copy in spread_tok(final_ref, (tok,), final_send, final_recv):
        copy.wait()
    for k in range(req_dev):
        wanted = ((tok * SIDE * SIDE + voc) * req_dev + k).astype(jnp.float32)
        for kind in range(2):
            found = jnp.zeros((8, 128), jnp.float32)
            for t in range(n_tok):
                found = found + jnp.where(owner_ref[t] == wanted, final_ref[t, kind], 0.0)
            found = jnp.sum(found, axis=0, keepdims=True)
            out_ref[pl.ds(kind * req_dev + k, 1), :] = sum(found[:, part * span:(part + 1) * span] for part in range(128 // span))


def shards(n_tok, columns, hidden, norm_gain, head_weight, lengths, offsets, slot_request, targets):
    req_dev, span, width = hidden.shape
    vocab_dev = head_weight.shape[1]
    chunks = vocab_dev // columns
    line_rows = SIDE * req_dev * LIVE
    f32 = jnp.float32
    vmem = pl.BlockSpec(memory_space=pltpu.VMEM)
    dma = pltpu.SemaphoreType.DMA
    scores = pl.pallas_call(
        functools.partial(kernel, n_tok, columns),
        out_shape=jax.ShapeDtypeStruct((2 * req_dev, span), f32),
        in_specs=[pl.BlockSpec(memory_space=pl.ANY)] * 7,
        out_specs=vmem,
        scratch_shapes=[
            pltpu.VMEM(hidden.shape, hidden.dtype),
            pltpu.VMEM((1, width), f32),
            pltpu.VMEM(targets.shape, jnp.int32),
            pltpu.SMEM(lengths.shape, jnp.int32),
            pltpu.SMEM(offsets.shape, jnp.int32),
            pltpu.SMEM(slot_request.shape, jnp.int32),
            dma((6,)),
            pltpu.VMEM((req_dev * span, width), jnp.bfloat16),
            pltpu.VMEM((SIDE * line_rows, width), jnp.bfloat16),
            pltpu.VMEM((SIDE, SIDE, 8, 128), f32),
            pltpu.VMEM((chunks, width, columns), jnp.bfloat16),
            pltpu.VMEM((line_rows, columns), f32),
            pltpu.VMEM((line_rows, columns), f32),
            pltpu.VMEM((SIDE * 256, 128), f32),
            pltpu.VMEM((SIDE * 256, 128), f32),
            pltpu.VMEM((SIDE * 256, 128), f32),
            pltpu.VMEM((SIDE * 256, 128), f32),
            pltpu.VMEM((SIDE * 256, 128), jnp.int32),
            pltpu.VMEM((SIDE, 8, 128), f32),
            pltpu.VMEM((SIDE * SIDE, SIDE, 8, 128), f32),
            pltpu.VMEM((8, 128), f32),
            pltpu.VMEM((n_tok, 2, 8, 128), f32),
            pltpu.VMEM((n_tok, 8, 128), f32),
            dma((chunks,)),
            dma((16,)), dma((16,)), dma((6,)), dma((6,)),
            dma((1,)), dma((1,)), dma((n_tok,)), dma((n_tok,)), dma((n_tok,)), dma((n_tok,)),
        ],
        compiler_params=pltpu.CompilerParams(
            collective_id=0, has_side_effects=True, vmem_limit_bytes=58 * 2**20
        ),
        name="score",
    )(hidden, norm_gain.reshape(1, width), targets, lengths, offsets, slot_request, head_weight)
    return scores[:req_dev], scores[req_dev:]


def solution(mesh, columns=1280):
    placed = (
        P(("tok", "voc"), None, None),
        P(),
        P(None, "voc"),
        P(("tok", "voc")),
        P(("tok", "voc")),
        P(),
        P(("tok", "voc"), None),
    )
    return jax.shard_map(
        functools.partial(shards, mesh.shape["tok"], columns),
        mesh=mesh,
        in_specs=placed,
        out_specs=(P(("tok", "voc"), None), P(("tok", "voc"), None)),
        check_vma=False,
    )
```

```python
import functools

import jax
import jax.numpy as jnp
from jax import lax
from jax.experimental import pallas as pl
from jax.experimental.pallas import tpu as pltpu
from jax.sharding import PartitionSpec as P

EPS = 1e-06
LIVE = 24
SIDE = 4
LOW = -1e30
MESH = pl.DeviceIdType.MESH


def kernel(
    n_tok, columns,
    hidden_hbm, gain_hbm, targets_hbm, lengths_hbm, offsets_hbm, request_hbm, weight_hbm,
    out_ref,
    hidden_ref, gain_ref, targets_ref, lengths_ref, offsets_ref, request_ref, input_sem,
    normed_ref, rows_ref, meta_ref, weight_ref, even_ref, odd_ref,
    peak_ref, sum_ref, dot_ref, pick_ref, goal_ref,
    stat_ref, every_ref, code_ref, final_ref, owner_ref,
    weight_sem, row_send, row_recv, meta_send, meta_recv,
    stat_send, stat_recv, owner_send, owner_recv, final_send, final_recv,
):
    req_dev, span, width = hidden_hbm.shape
    vocab_dev = weight_hbm.shape[1]
    chunks = vocab_dev // columns
    shard_rows = req_dev * LIVE
    tok, voc = lax.axis_index("tok"), lax.axis_index("voc")
    core = lax.rem(tok, 2)
    high, low = voc // SIDE, lax.rem(voc, SIDE)
    a = low + core * (high - low)
    b = high + core * (low - high)

    def shard_of(b_at, a_at):
        high_at = b_at + core * (a_at - b_at)
        low_at = a_at + core * (b_at - a_at)
        return high_at * SIDE + low_at

    def ring(place, step):
        return lax.rem(place + step + SIDE, SIDE)

    a_next, a_prev, a_far = ring(a, 1), ring(a, -1), ring(a, 2)
    b_next, b_prev, b_far = ring(b, 1), ring(b, -1), ring(b, 2)
    mine = b * SIDE + a

    pairs = (
        (hidden_hbm, hidden_ref), (gain_hbm, gain_ref), (targets_hbm, targets_ref),
        (lengths_hbm, lengths_ref), (offsets_hbm, offsets_ref), (request_hbm, request_ref),
    )
    inputs = [pltpu.make_async_copy(src, dst, input_sem.at[n]) for n, (src, dst) in enumerate(pairs)]
    for copy in inputs:
        copy.start()

    barrier = pltpu.get_barrier_semaphore()
    to_a_next, to_a_prev = (tok, shard_of(b, a_next)), (tok, shard_of(b, a_prev))
    to_b_next, to_b_prev = (tok, shard_of(b_next, a)), (tok, shard_of(b_prev, a))
    for peer in (to_a_next, to_a_prev, to_b_next, to_b_prev):
        pl.semaphore_signal(barrier, inc=1, device_id=peer, device_id_type=MESH)
    for step in range(1, n_tok):
        pl.semaphore_signal(barrier, inc=1, device_id=(lax.rem(tok + step, n_tok), voc), device_id_type=MESH)

    weight_copies = [
        pltpu.make_async_copy(weight_hbm.at[:, pl.ds(c * columns, columns)], weight_ref.at[c], weight_sem.at[c])
        for c in range(chunks)
    ]
    for copy in weight_copies:
        copy.start()

    for copy in inputs:
        copy.wait()

    lane = lax.broadcasted_iota(jnp.int32, (1, 128), 1)
    which = lax.rem(lane // span, req_dev)
    own_half = lane // (req_dev * span) == lax.rem(a, 2)
    offset = jnp.where(which == 0, offsets_ref[0], offsets_ref[1])
    length = jnp.where(which == 0, lengths_ref[0], lengths_ref[1])
    relative = lax.rem(lane, span) - offset
    alive = own_half & (relative >= 0) & (relative < length)
    code = jnp.where(alive, (lane // span) * span + relative + 1, 0)
    first_slot = (tok * SIDE * SIDE + voc) * req_dev
    request = jnp.where(own_half, jnp.where(which == 0, request_ref[first_slot], request_ref[first_slot + 1]), 0)
    goals = targets_ref[...]
    goals = jnp.concatenate([goals[0:1], goals[1:2], goals[0:1], goals[1:2]], axis=1)
    goals = jnp.where(own_half, goals, 0)
    meta_ref[b, a] = jnp.concatenate(
        [goals.astype(jnp.float32), code.astype(jnp.float32), request.astype(jnp.float32), jnp.zeros((5, 128), jnp.float32)], axis=0
    )

    for j in range(req_dev):
        values = hidden_ref[j].astype(jnp.float32)
        square = jnp.mean(values * values, axis=-1, keepdims=True)
        normed_ref[pl.ds(j * span, span), :] = (values * lax.rsqrt(square + EPS) * gain_ref[...]).astype(jnp.bfloat16)
    row = lax.broadcasted_iota(jnp.int32, (shard_rows, req_dev * span), 0)
    column = lax.broadcasted_iota(jnp.int32, (shard_rows, req_dev * span), 1)
    source = jnp.where(row < LIVE, row + offsets_ref[0], row - LIVE + span + offsets_ref[1])
    chosen = jnp.where(source == column, 1.0, 0.0).astype(jnp.bfloat16)
    rows_ref[pl.ds(0, shard_rows), :] = jnp.dot(
        chosen, normed_ref[...], preferred_element_type=jnp.float32
    ).astype(jnp.bfloat16)
    peak_ref[...] = jnp.full_like(peak_ref, LOW)
    sum_ref[...] = jnp.zeros_like(sum_ref)
    dot_ref[...] = jnp.zeros_like(dot_ref)
    pick_ref[...] = jnp.zeros_like(pick_ref)

    line_rows = SIDE * shard_rows
    sub_row = lax.broadcasted_iota(jnp.int32, (128, 128), 0).astype(jnp.float32) + 1.0
    sub_lane = lax.broadcasted_iota(jnp.int32, (128, 128), 1)
    lines = (b, b_next, b_prev, b_far)
    a_order = (a, a_next, a_far, a_prev)
    buffers = (even_ref, odd_ref)
    blocks = ((0, shard_rows), (shard_rows, 3 * shard_rows), (line_rows, 2 * line_rows), (3 * line_rows, line_rows))
    sends = []

    def push(ref, source, target, sems, place, peer):
        copy = pltpu.make_async_remote_copy(
            src_ref=ref.at[source], dst_ref=ref.at[target], send_sem=sems[0].at[place], recv_sem=sems[1].at[place],
            device_id=peer, device_id_type=MESH,
        )
        copy.start()
        sends.append(copy)
        return copy

    def landed(ref, index, sems, place):
        pltpu.make_async_copy(ref.at[index], ref.at[index], sems[1].at[place]).wait()

    row_sems, meta_sems = (row_send, row_recv), (meta_send, meta_recv)
    whole, left, right = pl.ds(0, width), pl.ds(0, width // 2), pl.ds(width // 2, width // 2)

    def shard(line, place, part=whole):
        return (pl.ds(line * line_rows + place * shard_rows, shard_rows), part)

    def whole_line(line, part):
        return (pl.ds(line * line_rows, line_rows), part)

    def goals_of(position):
        line = lines[position]
        for half in range(2):
            both = meta_ref[line, 2 * half] + meta_ref[line, 2 * half + 1]
            goal = jnp.sum(jnp.where(both[1:2] == sub_row, both[0:1], 0.0), axis=1, keepdims=True)
            at = pl.ds(position * 256 + half * 128, 128)
            goal_ref[at, :] = goal.astype(jnp.int32) - voc * vocab_dev - sub_lane

    def own_goals():
        both = meta_ref[b, a]
        for half in range(2):
            goal = jnp.sum(jnp.where(both[1:2] == sub_row, both[0:1], 0.0), axis=1, keepdims=True)
            goal_ref[pl.ds(half * 128, 128), :] = goal.astype(jnp.int32) - voc * vocab_dev - sub_lane

    def multiply(block, chunk, buffer):
        start, count = blocks[block]
        buffer[pl.ds(0, count), :] = jnp.dot(
            rows_ref[pl.ds(start, count), :], weight_ref[chunk], preferred_element_type=jnp.float32
        )

    def collect(block, chunk, buffer):
        start, count = blocks[block]
        for group in range(count // 8):
            flat = start + group * 8
            position, place = flat // line_rows, flat % line_rows // shard_rows
            request_at, part = flat % shard_rows // LIVE, flat % LIVE
            base = position * 256 + request_at * span + part
            at = pl.ds(pl.multiple_of(a_order[place] * (req_dev * span) + base, 8), 8)
            logits = [buffer[pl.ds(group * 8, 8), pl.ds(c * 128, 128)] for c in range(columns // 128)]
            peak = peak_ref[at]
            top = functools.reduce(jnp.maximum, logits, peak)
            rescale = jnp.exp(peak - top)
            exp_sum, exp_dot = sum_ref[at] * rescale, dot_ref[at] * rescale
            picked, goal = pick_ref[at], goal_ref[at]
            for c, logit in enumerate(logits):
                scaled = jnp.exp(logit - top)
                exp_sum = exp_sum + scaled
                exp_dot = exp_dot + scaled * logit
                picked = jnp.where(goal == chunk * columns + c * 128, logit, picked)
            peak_ref[at], sum_ref[at], dot_ref[at], pick_ref[at] = top, exp_sum, exp_dot, picked

    def finish(position):
        for half in range(2):
            at = pl.ds(position * 256 + half * 128, 128)
            peak = peak_ref[at].T
            top = jnp.max(peak, axis=0, keepdims=True)
            rescale = jnp.exp(peak - top)
            stat_ref[position, pl.ds(half, 1), :] = top
            stat_ref[position, pl.ds(2 + half, 1), :] = jnp.sum(sum_ref[at].T * rescale, axis=0, keepdims=True)
            stat_ref[position, pl.ds(4 + half, 1), :] = jnp.sum(dot_ref[at].T * rescale, axis=0, keepdims=True)
            stat_ref[position, pl.ds(6 + half, 1), :] = jnp.sum(pick_ref[at].T, axis=0, keepdims=True)

    far_first = sorted(
        ((i, j) for i in range(SIDE) for j in range(SIDE) if i or j), key=lambda s: -(min(s[0], SIDE - s[0]) + min(s[1], SIDE - s[1]))
    )

    def spread(position):
        for i, j in far_first:
            pltpu.make_async_remote_copy(
                src_ref=stat_ref.at[position], dst_ref=every_ref.at[mine, lines[position]],
                send_sem=stat_send.at[0], recv_sem=stat_recv.at[0],
                device_id=(tok, shard_of(ring(b, i), ring(a, j))), device_id_type=MESH,
            ).start()
        every_ref[mine, lines[position]] = stat_ref[position]

    def spread_tok(ref, index, send_sem, recv_sem):
        copies = []
        for step in sorted(range(1, n_tok), key=lambda k: -min(k, n_tok - k)):
            copy = pltpu.make_async_remote_copy(
                src_ref=ref.at[index], dst_ref=ref.at[index], send_sem=send_sem.at[step], recv_sem=recv_sem.at[step],
                device_id=(lax.rem(tok + step, n_tok), voc), device_id_type=MESH,
            )
            copy.start()
            copies.append(copy)
        return copies

    def steps(block, first):
        one, two = buffers[first], buffers[1 - first]

        @pl.loop(0, (chunks - 1) // 2)
        def _(pair):
            multiply(block, 2 * pair + 1, two)
            collect(block, 2 * pair, one)
            multiply(block, 2 * pair + 2, one)
            collect(block, 2 * pair + 1, two)

    pl.semaphore_wait(barrier, 4 + n_tok - 1)
    own_next = push(rows_ref, shard(0, 0), shard(0, 3), row_sems, 0, to_a_next)
    own_prev = push(rows_ref, shard(0, 0), shard(0, 1), row_sems, 1, to_a_prev)
    push(meta_ref, (b, a), (b, a), meta_sems, 0, to_a_next)
    push(meta_ref, (b, a), (b, a), meta_sems, 1, to_a_prev)
    own_goals()

    for chunk in range(chunks):
        weight_copies[chunk].wait()
        multiply(0, chunk, buffers[chunk % 2])
        if chunk > 0:
            collect(0, chunk - 1, buffers[1 - chunk % 2])
        if chunk == min(1, chunks - 1):
            own_next.wait_send()
            own_prev.wait_send()
            push(rows_ref, shard(0, 0), shard(2, 0), row_sems, 4, to_b_next)
            push(rows_ref, shard(0, 0), shard(1, 0), row_sems, 5, to_b_prev)
        if chunk == min(2, chunks - 1):
            landed(rows_ref, shard(0, 3), row_sems, 0)
            push(rows_ref, shard(0, 3, left), shard(0, 2, left), row_sems, 2, to_a_next)
            landed(rows_ref, shard(0, 1), row_sems, 1)
            push(rows_ref, shard(0, 1, right), shard(0, 2, right), row_sems, 3, to_a_prev)
            landed(meta_ref, (b, a_prev), meta_sems, 0)
            push(meta_ref, (b, a_prev), (b, a_prev), meta_sems, 2, to_a_next)
            landed(meta_ref, (b, a_next), meta_sems, 1)
            for k, place in enumerate((1, 3)):
                push(rows_ref, shard(0, place), shard(2, place), row_sems, 6 + 2 * k, to_b_next)
                push(rows_ref, shard(0, place), shard(1, place), row_sems, 7 + 2 * k, to_b_prev)
    landed(rows_ref, shard(0, 2, left), row_sems, 2)
    landed(rows_ref, shard(0, 2, right), row_sems, 3)
    push(rows_ref, shard(0, 2), shard(2, 2), row_sems, 10, to_b_next)
    push(rows_ref, shard(0, 2), shard(1, 2), row_sems, 11, to_b_prev)
    landed(meta_ref, (b, a_far), meta_sems, 2)
    push(meta_ref, (b,), (b,), meta_sems, 3, to_b_next)
    push(meta_ref, (b,), (b,), meta_sems, 4, to_b_prev)

    at_chunk = (chunks - 1) % 2
    multiply(1, 0, buffers[1 - at_chunk])
    collect(0, chunks - 1, buffers[at_chunk])
    goals_of(0)
    first = 1 - at_chunk
    steps(1, first)
    for k, place in enumerate((0, 1, 3, 2)):
        landed(rows_ref, shard(2, place), row_sems, 4 + 2 * k)
        landed(rows_ref, shard(1, place), row_sems, 5 + 2 * k)
    push(rows_ref, whole_line(2, left), whole_line(3, left), row_sems, 12, to_b_next)
    push(rows_ref, whole_line(1, right), whole_line(3, right), row_sems, 13, to_b_prev)
    landed(meta_ref, (b_prev,), meta_sems, 3)
    landed(meta_ref, (b_next,), meta_sems, 4)
    push(meta_ref, (b_prev,), (b_prev,), meta_sems, 5, to_b_next)
    multiply(2, 0, buffers[1 - first])
    collect(1, chunks - 1, buffers[first])
    finish(0)
    goals_of(1)
    goals_of(2)
    first = 1 - first
    steps(2, first)
    landed(rows_ref, whole_line(3, left), row_sems, 12)
    landed(rows_ref, whole_line(3, right), row_sems, 13)
    landed(meta_ref, (b_far,), meta_sems, 5)
    multiply(3, 0, buffers[1 - first])
    collect(2, chunks - 1, buffers[first])
    goals_of(3)
    finish(1)
    finish(2)
    for position in range(3):
        spread(position)
    for line in range(SIDE):
        for half in range(2):
            both = meta_ref[line, 2 * half] + meta_ref[line, 2 * half + 1]
            code_ref[pl.ds(2 * line + half, 1), :] = both[1:2]
            owner_ref[tok, pl.ds(2 * line + half, 1), :] = both[2:3]
    owner_copies = spread_tok(owner_ref, (tok,), owner_send, owner_recv)
    first = 1 - first
    steps(3, first)
    collect(3, chunks - 1, buffers[first])
    finish(3)
    spread(3)
    for copy in sends:
        if copy is not own_next and copy is not own_prev:
            copy.wait_send()
    for copy in owner_copies:
        copy.wait()
    others = every_ref.at[pl.ds(0, SIDE * SIDE - 1)]
    pltpu.make_async_copy(others, others, stat_recv.at[0]).wait()
    pltpu.make_async_copy(others, others, stat_send.at[0]).wait()

    peers = range(SIDE * SIDE)
    for line in range(SIDE):
        peaks = [every_ref[s, line, pl.ds(0, 2), :] for s in peers]
        top = functools.reduce(jnp.maximum, peaks)
        exp_sum = exp_dot = picked = jnp.zeros((2, 128), jnp.float32)
        for s in peers:
            rescale = jnp.exp(peaks[s] - top)
            exp_sum = exp_sum + every_ref[s, line, pl.ds(2, 2), :] * rescale
            exp_dot = exp_dot + every_ref[s, line, pl.ds(4, 2), :] * rescale
            picked = picked + every_ref[s, line, pl.ds(6, 2), :]
        log_total = jnp.log(exp_sum)
        final_ref[tok, 0, pl.ds(2 * line, 2), :] = picked - top - log_total
        final_ref[tok, 1, pl.ds(2 * line, 2), :] = top + log_total - exp_dot / exp_sum
    code = code_ref[...].astype(jnp.int32)
    shift = jnp.where(code > 0, lax.broadcasted_iota(jnp.int32, (8, 128), 1) + 1 - code, -1)
    for kind in range(2):
        score = final_ref[tok, kind]
        placed = jnp.zeros((8, 128), jnp.float32)
        for amount in range(span - LIVE + 1):
            moved = score if amount == 0 else pltpu.roll(score, amount, 1)
            placed = jnp.where(shift == amount, moved, placed)
        final_ref[tok, kind] = placed
    for copy in spread_tok(final_ref, (tok,), final_send, final_recv):
        copy.wait()
    for k in range(req_dev):
        wanted = ((tok * SIDE * SIDE + voc) * req_dev + k).astype(jnp.float32)
        for kind in range(2):
            found = jnp.zeros((8, 128), jnp.float32)
            for t in range(n_tok):
                found = found + jnp.where(owner_ref[t] == wanted, final_ref[t, kind], 0.0)
            found = jnp.sum(found, axis=0, keepdims=True)
            out_ref[pl.ds(kind * req_dev + k, 1), :] = sum(found[:, part * span:(part + 1) * span] for part in range(128 // span))


def shards(n_tok, columns, hidden, norm_gain, head_weight, lengths, offsets, slot_request, targets):
    req_dev, span, width = hidden.shape
    vocab_dev = head_weight.shape[1]
    chunks = vocab_dev // columns
    line_rows = SIDE * req_dev * LIVE
    f32 = jnp.float32
    vmem = pl.BlockSpec(memory_space=pltpu.VMEM)
    dma = pltpu.SemaphoreType.DMA
    scores = pl.pallas_call(
        functools.partial(kernel, n_tok, columns),
        out_shape=jax.ShapeDtypeStruct((2 * req_dev, span), f32),
        in_specs=[pl.BlockSpec(memory_space=pl.ANY)] * 7,
        out_specs=vmem,
        scratch_shapes=[
            pltpu.VMEM(hidden.shape, hidden.dtype),
            pltpu.VMEM((1, width), f32),
            pltpu.VMEM(targets.shape, jnp.int32),
            pltpu.SMEM(lengths.shape, jnp.int32),
            pltpu.SMEM(offsets.shape, jnp.int32),
            pltpu.SMEM(slot_request.shape, jnp.int32),
            dma((6,)),
            pltpu.VMEM((req_dev * span, width), jnp.bfloat16),
            pltpu.VMEM((SIDE * line_rows, width), jnp.bfloat16),
            pltpu.VMEM((SIDE, SIDE, 8, 128), f32),
            pltpu.VMEM((chunks, width, columns), jnp.bfloat16),
            pltpu.VMEM((2 * line_rows, columns), f32),
            pltpu.VMEM((2 * line_rows, columns), f32),
            pltpu.VMEM((SIDE * 256, 128), f32),
            pltpu.VMEM((SIDE * 256, 128), f32),
            pltpu.VMEM((SIDE * 256, 128), f32),
            pltpu.VMEM((SIDE * 256, 128), f32),
            pltpu.VMEM((SIDE * 256, 128), jnp.int32),
            pltpu.VMEM((SIDE, 8, 128), f32),
            pltpu.VMEM((SIDE * SIDE, SIDE, 8, 128), f32),
            pltpu.VMEM((8, 128), f32),
            pltpu.VMEM((n_tok, 2, 8, 128), f32),
            pltpu.VMEM((n_tok, 8, 128), f32),
            dma((chunks,)),
            dma((14,)), dma((14,)), dma((6,)), dma((6,)),
            dma((1,)), dma((1,)), dma((n_tok,)), dma((n_tok,)), dma((n_tok,)), dma((n_tok,)),
        ],
        compiler_params=pltpu.CompilerParams(
            collective_id=0, has_side_effects=True, vmem_limit_bytes=58 * 2**20
        ),
        name="score",
    )(hidden, norm_gain.reshape(1, width), targets, lengths, offsets, slot_request, head_weight)
    return scores[:req_dev], scores[req_dev:]


def solution(mesh, columns=1280):
    placed = (
        P(("tok", "voc"), None, None),
        P(),
        P(None, "voc"),
        P(("tok", "voc")),
        P(("tok", "voc")),
        P(),
        P(("tok", "voc"), None),
    )
    return jax.shard_map(
        functools.partial(shards, mesh.shape["tok"], columns),
        mesh=mesh,
        in_specs=placed,
        out_specs=(P(("tok", "voc"), None), P(("tok", "voc"), None)),
        check_vma=False,
    )
```
